256 devices in a mesh: dp: 16 (over z_hi, y, core), bulk: 16 (over x, z_lo).
Axes of the slice: x: 4, y: 4, z: 8 (z_hi: 2, z_lo: 4; z = z_hi * 4 + z_lo), core: 2. Of those that a mesh axis runs over, the one named last changes fastest.
Arguments:
- node_feats: bfloat16 [196608, 512], P(('dp', 'bulk')), may hold values from -6 to 6
- edge_feats: bfloat16 [262144, 512], P(('dp', 'bulk')), may hold values from -6 to 6
- grad_nodes: bfloat16 [196608, 512], P(('dp', 'bulk')), may hold values from -6 to 6
- grad_edges: bfloat16 [262144, 512], P(('dp', 'bulk')), may hold values from -6 to 6
- sources: int32 [262144], P(('dp', 'bulk')), may hold values from 0 to 1023
- tile_blocks: int32 [2048], P(('dp', 'bulk')), may hold values from 0 to 5
- offsets: int32 [262144], P(('dp', 'bulk')), may hold values from 0 to 127
- edge_count: int32 [256], P(('dp', 'bulk')), may hold values from 512 to 1024, as said below
- weights: bfloat16 [3584, 512], replicated
Outputs:
- node_grads: bfloat16 [196608, 512], P(('dp', 'bulk'))
- edge_grads: bfloat16 [262144, 512], P(('dp', 'bulk'))
- weight_grads: float32 [3584, 512], P('dp')
The draws below stay inside these ranges and needn't reach their ends.
Inputs may be any that keep to these rules, and one draw needn't show every extreme that they name: `sources`: rows 0 to 127 and the last 128 rows of a slab's extended list are the neighbours' boundary nodes. `edge_count`: some slab is full in every draw.
All inputs are finite; a program needn't handle non-finite values.
Results may differ from the reference program's by a relative error of at most 0.0065.
Values may be sent and summed in bfloat16 or wider, within the bound.
A program may use at most 128 MiB of HBM per device.

```python
import jax
import jax.numpy as jnp
from jax import lax

H = 512
TILE = 128
HALO = 128
N_OWN = 768
E_DEV = 1024
NB = 6
TILES = 8
SLABS = 256
NODES = 196608
EDGES = 262144
ALLTILES = 2048
N_DP = 16
N_BULK = 16


def draw_edge_count(key, part):
    counts = jax.random.randint(key, (SLABS,), E_DEV // 2, E_DEV + 1)
    fullest = jax.random.randint(jax.random.fold_in(key, 7), (), 0, SLABS)
    return counts.at[fullest].set(E_DEV).astype(jnp.int32)


def draw_weights(key, part):
    values = jax.random.normal(key, (7 * H, H), jnp.float32)
    rows = jnp.arange(7 * H)[:, None]
    scale = jnp.where(rows < 3 * H, (3.0 * H) ** (-0.5), jnp.where(rows < 4 * H, (1.0 * H) ** (-0.5), jnp.where(rows < 6 * H, (2.0 * H) ** (-0.5), (1.0 * H) ** (-0.5))))
    return (values * scale).astype(jnp.bfloat16)


def touch_ends(result, stream_key, least, largest):
    index_at = [jax.random.randint(jax.random.fold_in(stream_key, axis), (), 0, length) for axis, length in enumerate(result.shape)]
    main_axis = result.shape.index(max(result.shape))
    beside = index_at[:main_axis] + [(index_at[main_axis] + 1) % result.shape[main_axis]] + index_at[main_axis + 1:]
    return result.at[tuple(index_at)].set(least).at[tuple(beside)].set(largest)


def shard_levels(key, dims, shards, least, high):
    loudness, own = 1.0, jax.random.fold_in(key, 6)
    for position, blocks in shards:
        heights = jnp.exp(jax.random.uniform(jax.random.fold_in(own, position), (blocks,), jnp.float32, least / len(shards), high / len(shards)))
        loudness = loudness * jnp.repeat(heights, dims[position] // blocks).reshape([-1 if axis == position else 1 for axis in range(len(dims))])
    return loudness


def normal_values(own_key, extent, scale, reach, pieces=(), kind=jnp.bfloat16):
    values = jax.random.normal(own_key, extent, jnp.float32) * scale
    if len(pieces) > 0:
        values = shard_levels(own_key, extent, pieces, -0.22, 0.18) * values
    return jnp.clip(values, min=-reach, max=reach).astype(kind)


def setup_inputs(seed: int = 0) -> dict:
    arg_keys = jax.random.split(jax.random.key(seed), 10)
    node_feats = normal_values(arg_keys[0], (NODES, H), 1.0, 6.0, ((0, 256),))
    edge_feats = normal_values(arg_keys[1], (EDGES, H), 1.0, 6.0, ((0, 256),))
    grad_nodes = normal_values(arg_keys[2], (NODES, H), 1.0, 6.0, ((0, 256),))
    grad_edges = normal_values(arg_keys[3], (EDGES, H), 1.0, 6.0, ((0, 256),))
    sources = touch_ends(jax.random.randint(arg_keys[4], (EDGES,), 0, N_OWN + 2 * HALO), jax.random.fold_in(arg_keys[4], 1), 0, (N_OWN + 2 * HALO) - 1).astype(jnp.int32)
    tile_blocks = touch_ends(jax.random.randint(arg_keys[5], (ALLTILES,), 0, NB), jax.random.fold_in(arg_keys[5], 1), 0, NB - 1).astype(jnp.int32)
    offsets = touch_ends(jax.random.randint(arg_keys[6], (EDGES,), 0, TILE), jax.random.fold_in(arg_keys[6], 1), 0, TILE - 1).astype(jnp.int32)
    edge_count = draw_edge_count(jax.random.fold_in(arg_keys[9], 71), 0)
    weights = draw_weights(jax.random.fold_in(arg_keys[9], 71), 0)
    return dict(node_feats=node_feats, edge_feats=edge_feats, grad_nodes=grad_nodes, grad_edges=grad_edges, sources=sources, tile_blocks=tile_blocks, offsets=offsets, edge_count=edge_count, weights=weights)


def ln_core(values):
    middle = values - lax.optimization_barrier(jnp.mean(values, -1, keepdims=True))
    spread = lax.optimization_barrier(jnp.mean(middle * middle, -1, keepdims=True))
    return middle * lax.rsqrt(spread + 1e-05)

def ln_back(values, cotangent):
    unused, pull = jax.vjp(ln_core, values)
    return pull(cotangent)[0]

def silu_back(values, cotangent):
    sigma = jax.nn.sigmoid(values)
    return cotangent * sigma * (1.0 + values * (1.0 - sigma))

def left_dot(first, second):
    return lax.dot_general(first, second, (((0,), (0,)), ((), ())), preferred_element_type=jnp.float32)

def right_dot(first, second):
    return lax.dot_general(first, second, (((1,), (1,)), ((), ())), preferred_element_type=jnp.float32)

def slab_backward(extended, edge_feats, grad_nodes, grad_edges, sources, tile_blocks, offsets, count, weights):
    width = weights.shape[1]
    own_rows = grad_nodes.shape[0]
    rim = (extended.shape[0] - own_rows) // 2
    ntiles = tile_blocks.shape[0]
    nedges = offsets.shape[0]
    tile = nedges // ntiles
    nblocks = own_rows // tile
    w_edge_one = weights[:3 * width]
    w_edge_two = weights[3 * width:4 * width]
    w_node_one = weights[4 * width:6 * width]
    w_node_two = weights[6 * width:]
    dest = (jnp.repeat(tile_blocks, tile) * tile + offsets).astype(jnp.int32)
    live = (jnp.arange(nedges) < count).astype(jnp.float32)[:, None]
    joined = jnp.concatenate([extended[sources], extended[dest + rim], edge_feats], 1)
    act_one = jnp.dot(joined, w_edge_one, preferred_element_type=jnp.float32)
    hidden_one = jax.nn.silu(act_one).astype(jnp.bfloat16)
    act_two = jnp.dot(hidden_one, w_edge_two, preferred_element_type=jnp.float32)
    message = (ln_core(act_two) * live).astype(jnp.bfloat16)
    onehot = (offsets.reshape(ntiles, tile)[:, :, None] == jnp.arange(tile)[None, None, :]).astype(jnp.bfloat16)
    pertile = jnp.einsum('tek,teh->tkh', onehot, message.reshape(ntiles, tile, width), preferred_element_type=jnp.float32)
    gathered = jnp.zeros((nblocks, tile, width), jnp.float32).at[tile_blocks].add(pertile)
    aggregate = gathered.reshape(own_rows, width).astype(jnp.bfloat16)
    own_feats = extended[rim:rim + own_rows]
    joined_nodes = jnp.concatenate([own_feats, aggregate], 1)
    node_one = jnp.dot(joined_nodes, w_node_one, preferred_element_type=jnp.float32)
    node_hidden = jax.nn.silu(node_one).astype(jnp.bfloat16)
    node_two = jnp.dot(node_hidden, w_node_two, preferred_element_type=jnp.float32)
    d_node_two = ln_back(node_two, grad_nodes.astype(jnp.float32)).astype(jnp.bfloat16)
    g_node_two = left_dot(node_hidden, d_node_two)
    d_node_one = silu_back(node_one, right_dot(d_node_two, w_node_two)).astype(jnp.bfloat16)
    g_node_one = left_dot(joined_nodes, d_node_one)
    d_inputs = right_dot(d_node_one, w_node_one)
    d_aggregate = d_inputs[:, width:].astype(jnp.bfloat16)
    pulled = d_aggregate.reshape(nblocks, tile, width)[tile_blocks]
    d_message = jnp.einsum('tek,tkh->teh', onehot, pulled, preferred_element_type=jnp.float32).reshape(nedges, width)
    d_msg_total = live * (d_message + grad_edges.astype(jnp.float32))
    d_act_two = ln_back(act_two, d_msg_total).astype(jnp.bfloat16)
    g_edge_two = left_dot(hidden_one, d_act_two)
    d_act_one = silu_back(act_one, right_dot(d_act_two, w_edge_two)).astype(jnp.bfloat16)
    g_edge_one = left_dot(joined, d_act_one)
    d_joined = right_dot(d_act_one, w_edge_one)
    edge_grads = (grad_edges.astype(jnp.float32) + d_joined[:, 2 * width:]).astype(jnp.bfloat16)
    d_extended = jnp.zeros((extended.shape[0], width), jnp.float32)
    d_extended = d_extended.at[sources].add(d_joined[:, :width])
    d_extended = d_extended.at[dest + rim].add(d_joined[:, width:2 * width])
    d_extended = d_extended.at[rim:rim + own_rows].add(grad_nodes.astype(jnp.float32) + d_inputs[:, :width])
    grads = jnp.concatenate([g_edge_one, g_edge_two, g_node_one, g_node_two], 0)
    return (d_extended, edge_grads, grads)

def reference(node_feats, edge_feats, grad_nodes, grad_edges, sources, tile_blocks, offsets, edge_count, weights):
    slabs = N_DP * N_BULK
    stacked = node_feats.reshape(N_DP, N_BULK, N_OWN, H)
    zero_rim = jnp.zeros((N_DP, 1, HALO, H), node_feats.dtype)
    before = jnp.concatenate([zero_rim, stacked[:, :-1, N_OWN - HALO:]], 1)
    after = jnp.concatenate([stacked[:, 1:, :HALO], zero_rim], 1)
    extended = jnp.concatenate([before, stacked, after], 2).reshape(slabs, N_OWN + 2 * HALO, H)
    inputs = (extended, edge_feats.reshape(slabs, E_DEV, H), grad_nodes.reshape(slabs, N_OWN, H), grad_edges.reshape(slabs, E_DEV, H), sources.reshape(slabs, E_DEV), tile_blocks.reshape(slabs, TILES), offsets.reshape(slabs, E_DEV), edge_count)

    def step(total, item):
        d_ext, e_grad, grads = slab_backward(item[0], item[1], item[2], item[3], item[4], item[5], item[6], item[7], weights)
        return (total + grads, (d_ext, e_grad))
    total, outs = lax.scan(step, jnp.zeros((7 * H, H), jnp.float32), inputs)
    d_ext = outs[0].reshape(N_DP, N_BULK, N_OWN + 2 * HALO, H)
    own = d_ext[:, :, HALO:HALO + N_OWN]
    zero_grad = jnp.zeros((N_DP, 1, HALO, H), jnp.float32)
    from_before = jnp.concatenate([zero_grad, d_ext[:, :-1, HALO + N_OWN:]], 1)
    from_after = jnp.concatenate([d_ext[:, 1:, :HALO], zero_grad], 1)
    own = own.at[:, :, :HALO].add(from_before)
    own = own.at[:, :, N_OWN - HALO:].add(from_after)
    node_grads = own.reshape(N_DP * N_BULK * N_OWN, H).astype(jnp.bfloat16)
    edge_grads = outs[1].reshape(N_DP * N_BULK * E_DEV, H)
    factor = 1.0 / jnp.sqrt(jnp.float32(N_DP * N_BULK * E_DEV))
    return (node_grads, edge_grads, total * factor)
```

```python
import jax
import jax.numpy as jnp
import numpy as np
from jax import lax
from jax.sharding import Mesh
from jax.sharding import PartitionSpec as P

HALO = 128


def extended_2(block, sides, width):
    for axis, dim in sides:
        count = axis_count(axis)
        forward = [(i, i + 1) for i in range(count - 1)]
        backward = [(target, source) for source, target in forward]
        low = lax.ppermute(
            lax.slice_in_dim(block, block.shape[dim] - width, None, axis=dim), axis, forward
        )
        high = lax.ppermute(lax.slice_in_dim(block, 0, width, axis=dim), axis, backward)
        block = jnp.concatenate([low, block, high], axis=dim)
    return block


def axis_count(axis):
    return int(np.prod([lax.axis_size(name) for name in axis]))


def shifted(value, axis, steps):
    count = axis_count(axis)
    initial, last = (max(0, -steps), min(count, count - steps))
    return lax.ppermute(value, axis, [(source, source + steps) for source in range(initial, last)])


def ln_core(values):
    middle = values - jnp.mean(values, -1, keepdims=True)
    spread = jnp.mean(middle * middle, -1, keepdims=True)
    return middle * lax.rsqrt(spread + 1e-05)


def ln_back(values, cotangent):
    unused, pull = jax.vjp(ln_core, values)
    return pull(cotangent)[0]


def silu_back(values, cotangent):
    sigma = jax.nn.sigmoid(values)
    return cotangent * sigma * (1.0 + values * (1.0 - sigma))


def left_dot(first, second):
    return lax.dot_general(
        first, second, (((0,), (0,)), ((), ())), preferred_element_type=jnp.float32
    )


def right_dot(first, second):
    return lax.dot_general(
        first, second, (((1,), (1,)), ((), ())), preferred_element_type=jnp.float32
    )


def slab_backward(
    extended, edge_feats, grad_nodes, grad_edges, sources, tile_blocks, offsets, count, weights
):
    width = weights.shape[1]
    own_rows = grad_nodes.shape[0]
    rim = (extended.shape[0] - own_rows) // 2
    ntiles = tile_blocks.shape[0]
    nedges = offsets.shape[0]
    tile = nedges // ntiles
    nblocks = own_rows // tile
    w_edge_one = weights[: 3 * width]
    w_edge_two = weights[3 * width : 4 * width]
    w_node_one = weights[4 * width : 6 * width]
    w_node_two = weights[6 * width :]
    dest = jnp.repeat(tile_blocks, tile) * tile + offsets
    live = (jnp.arange(nedges) < count).astype(jnp.float32)[:, None]
    joined = jnp.concatenate([extended[sources], extended[dest + rim], edge_feats], 1)
    act_one = jnp.dot(joined, w_edge_one, preferred_element_type=jnp.float32)
    hidden_one = jax.nn.silu(act_one).astype(jnp.bfloat16)
    act_two = jnp.dot(hidden_one, w_edge_two, preferred_element_type=jnp.float32)
    message = (ln_core(act_two) * live).astype(jnp.bfloat16)
    onehot = (offsets.reshape(ntiles, tile)[:, :, None] == jnp.arange(tile)[None, None, :]).astype(
        jnp.bfloat16
    )
    pertile = jnp.einsum(
        "tek,teh->tkh",
        onehot,
        message.reshape(ntiles, tile, width),
        preferred_element_type=jnp.float32,
    )
    gathered = jnp.zeros((nblocks, tile, width), jnp.float32).at[tile_blocks].add(pertile)
    aggregate = gathered.reshape(own_rows, width).astype(jnp.bfloat16)
    own_feats = extended[rim : rim + own_rows]
    joined_nodes = jnp.concatenate([own_feats, aggregate], 1)
    node_one = jnp.dot(joined_nodes, w_node_one, preferred_element_type=jnp.float32)
    node_hidden = jax.nn.silu(node_one).astype(jnp.bfloat16)
    node_two = jnp.dot(node_hidden, w_node_two, preferred_element_type=jnp.float32)
    d_node_two = ln_back(node_two, grad_nodes.astype(jnp.float32)).astype(jnp.bfloat16)
    g_node_two = left_dot(node_hidden, d_node_two)
    d_node_one = silu_back(node_one, right_dot(d_node_two, w_node_two)).astype(jnp.bfloat16)
    g_node_one = left_dot(joined_nodes, d_node_one)
    d_inputs = right_dot(d_node_one, w_node_one)
    d_aggregate = d_inputs[:, width:].astype(jnp.bfloat16)
    pulled = d_aggregate.reshape(nblocks, tile, width)[tile_blocks]
    d_message = jnp.einsum(
        "tek,tkh->teh", onehot, pulled, preferred_element_type=jnp.float32
    ).reshape(nedges, width)
    d_msg_total = live * (d_message + grad_edges.astype(jnp.float32))
    d_act_two = ln_back(act_two, d_msg_total).astype(jnp.bfloat16)
    g_edge_two = left_dot(hidden_one, d_act_two)
    d_act_one = silu_back(act_one, right_dot(d_act_two, w_edge_two)).astype(jnp.bfloat16)
    g_edge_one = left_dot(joined, d_act_one)
    d_joined = right_dot(d_act_one, w_edge_one)
    edge_grads = (grad_edges.astype(jnp.float32) + d_joined[:, 2 * width :]).astype(jnp.bfloat16)
    d_extended = jnp.zeros((extended.shape[0], width), jnp.float32)
    d_extended = d_extended.at[sources].add(d_joined[:, :width])
    d_extended = d_extended.at[dest + rim].add(d_joined[:, width : 2 * width])
    d_extended = d_extended.at[rim : rim + own_rows].add(
        grad_nodes.astype(jnp.float32) + d_inputs[:, :width]
    )
    grads = jnp.concatenate([g_edge_one, g_edge_two, g_node_one, g_node_two], 0)
    return (d_extended, edge_grads, grads)


DP = ("zh", "y", "c")
BULK = ("x", "zl")


def reduce_grads(grads):
    sizes = [lax.axis_size(name) for name in DP]
    rows = grads.shape[0] // int(np.prod(sizes))
    order = ("c", "y", "zh")
    blocks = grads.reshape(*sizes, rows, grads.shape[1])
    blocks = blocks.transpose([DP.index(name) for name in order] + [3, 4])
    part = blocks.reshape(grads.shape)
    for name in order + ("zl", "x"):
        part = lax.psum_scatter(part, name, scatter_dimension=0, tiled=True)
    for name in ("x", "zl"):
        part = lax.all_gather(part, name, axis=0, tiled=True)
    return part


def body(
    node_feats,
    edge_feats,
    grad_nodes,
    grad_edges,
    sources,
    tile_blocks,
    offsets,
    edge_count,
    weights,
):
    extended = extended_2(node_feats, ((BULK, 0),), HALO)
    d_extended, edge_grads, grads = slab_backward(
        extended,
        edge_feats,
        grad_nodes,
        grad_edges,
        sources,
        tile_blocks,
        offsets,
        edge_count[0],
        weights,
    )
    own_rows = node_feats.shape[0]
    from_after = shifted(d_extended[:HALO].astype(jnp.bfloat16), BULK, -1).astype(jnp.float32)
    from_before = shifted(d_extended[HALO + own_rows :].astype(jnp.bfloat16), BULK, 1).astype(
        jnp.float32
    )
    own = d_extended[HALO : HALO + own_rows]
    own = own.at[:HALO].add(from_before)
    own = own.at[own_rows - HALO :].add(from_after)
    node_grads = own.astype(jnp.bfloat16)
    summed = reduce_grads(grads)
    factor = 1.0 / jnp.sqrt(jnp.float32(axis_count(DP + BULK) * edge_feats.shape[0]))
    return (node_grads, edge_grads, summed * factor)


def solution(mesh):
    devices = np.asarray(mesh.devices)
    shape = (2, devices.shape[0] // 4, 2, devices.shape[1] // 4, 4)
    fine = Mesh(devices.reshape(shape), DP + BULK)
    rows = P(DP + BULK, None)
    flat = P(DP + BULK)
    in_specs = (rows, rows, rows, rows, flat, flat, flat, flat, P())
    out_specs = (rows, rows, P(DP, None))
    return jax.shard_map(body, mesh=fine, in_specs=in_specs, out_specs=out_specs, check_vma=False)
```

```python
import jax
import jax.numpy as jnp
import numpy as np
from jax import lax
from jax.sharding import Mesh
from jax.sharding import PartitionSpec as P

HALO = 128


def extended_2(block, sides, width):
    for axis, dim in sides:
        count = axis_count(axis)
        forward = [(i, i + 1) for i in range(count - 1)]
        backward = [(target, source) for source, target in forward]
        low = lax.ppermute(
            lax.slice_in_dim(block, block.shape[dim] - width, None, axis=dim), axis, forward
        )
        high = lax.ppermute(lax.slice_in_dim(block, 0, width, axis=dim), axis, backward)
        block = jnp.concatenate([low, block, high], axis=dim)
    return block


def axis_count(axis):
    return int(np.prod([lax.axis_size(name) for name in axis]))


def shifted(value, axis, steps):
    count = axis_count(axis)
    initial, last = (max(0, -steps), min(count, count - steps))
    return lax.ppermute(value, axis, [(source, source + steps) for source in range(initial, last)])


def ln_core(values):
    middle = values - jnp.mean(values, -1, keepdims=True)
    spread = jnp.mean(middle * middle, -1, keepdims=True)
    return middle * lax.rsqrt(spread + 1e-05)


def ln_back(values, cotangent):
    unused, pull = jax.vjp(ln_core, values)
    return pull(cotangent)[0]


def silu_back(values, cotangent):
    sigma = jax.nn.sigmoid(values)
    return cotangent * sigma * (1.0 + values * (1.0 - sigma))


def left_dot(first, second):
    return lax.dot_general(
        first, second, (((0,), (0,)), ((), ())), preferred_element_type=jnp.float32
    )


def right_dot(first, second):
    return lax.dot_general(
        first, second, (((1,), (1,)), ((), ())), preferred_element_type=jnp.float32
    )


def slab_backward(
    extended, edge_feats, grad_nodes, grad_edges, sources, tile_blocks, offsets, count, weights
):
    width = weights.shape[1]
    own_rows = grad_nodes.shape[0]
    rim = (extended.shape[0] - own_rows) // 2
    ntiles = tile_blocks.shape[0]
    nedges = offsets.shape[0]
    tile = nedges // ntiles
    nblocks = own_rows // tile
    w_edge_one = weights[: 3 * width]
    w_edge_two = weights[3 * width : 4 * width]
    w_node_one = weights[4 * width : 6 * width]
    w_node_two = weights[6 * width :]
    dest = jnp.repeat(tile_blocks, tile) * tile + offsets
    live = (jnp.arange(nedges) < count).astype(jnp.float32)[:, None]
    joined = jnp.concatenate([extended[sources], extended[dest + rim], edge_feats], 1)
    act_one = jnp.dot(joined, w_edge_one, preferred_element_type=jnp.float32)
    hidden_one = jax.nn.silu(act_one).astype(jnp.bfloat16)
    act_two = jnp.dot(hidden_one, w_edge_two, preferred_element_type=jnp.float32)
    message = (ln_core(act_two) * live).astype(jnp.bfloat16)
    onehot = (offsets.reshape(ntiles, tile)[:, :, None] == jnp.arange(tile)[None, None, :]).astype(
        jnp.bfloat16
    )
    pertile = jnp.einsum(
        "tek,teh->tkh",
        onehot,
        message.reshape(ntiles, tile, width),
        preferred_element_type=jnp.float32,
    )
    gathered = jnp.zeros((nblocks, tile, width), jnp.float32).at[tile_blocks].add(pertile)
    aggregate = gathered.reshape(own_rows, width).astype(jnp.bfloat16)
    own_feats = extended[rim : rim + own_rows]
    joined_nodes = jnp.concatenate([own_feats, aggregate], 1)
    node_one = jnp.dot(joined_nodes, w_node_one, preferred_element_type=jnp.float32)
    node_hidden = jax.nn.silu(node_one).astype(jnp.bfloat16)
    node_two = jnp.dot(node_hidden, w_node_two, preferred_element_type=jnp.float32)
    d_node_two = ln_back(node_two, grad_nodes.astype(jnp.float32)).astype(jnp.bfloat16)
    g_node_two = left_dot(node_hidden, d_node_two)
    d_node_one = silu_back(node_one, right_dot(d_node_two, w_node_two)).astype(jnp.bfloat16)
    g_node_one = left_dot(joined_nodes, d_node_one)
    d_inputs = right_dot(d_node_one, w_node_one)
    d_aggregate = d_inputs[:, width:].astype(jnp.bfloat16)
    pulled = d_aggregate.reshape(nblocks, tile, width)[tile_blocks]
    d_message = jnp.einsum(
        "tek,tkh->teh", onehot, pulled, preferred_element_type=jnp.float32
    ).reshape(nedges, width)
    d_msg_total = live * (d_message + grad_edges.astype(jnp.float32))
    d_act_two = ln_back(act_two, d_msg_total).astype(jnp.bfloat16)
    g_edge_two = left_dot(hidden_one, d_act_two)
    d_act_one = silu_back(act_one, right_dot(d_act_two, w_edge_two)).astype(jnp.bfloat16)
    g_edge_one = left_dot(joined, d_act_one)
    d_joined = right_dot(d_act_one, w_edge_one)
    edge_grads = (grad_edges.astype(jnp.float32) + d_joined[:, 2 * width :]).astype(jnp.bfloat16)
    d_extended = jnp.zeros((extended.shape[0], width), jnp.float32)
    d_extended = d_extended.at[sources].add(d_joined[:, :width])
    d_extended = d_extended.at[dest + rim].add(d_joined[:, width : 2 * width])
    d_extended = d_extended.at[rim : rim + own_rows].add(
        grad_nodes.astype(jnp.float32) + d_inputs[:, :width]
    )
    grads = jnp.concatenate([g_edge_one, g_edge_two, g_node_one, g_node_two], 0)
    return (d_extended, edge_grads, grads)


DP = ("zh", "y", "c")
BULK = ("x", "zl")


def reduce_grads(grads):
    gather = ("x", "zl")
    dims = DP + (gather[1], gather[0])
    sizes = [lax.axis_size(name) for name in dims]
    rows = grads.shape[0] // int(np.prod(sizes))
    order = ("c", "y", "x", "zl", "zh")
    blocks = grads.reshape(*sizes, rows, grads.shape[1])
    blocks = blocks.transpose([dims.index(name) for name in order] + [5, 6])
    part = blocks.reshape(grads.shape)
    for name in order:
        part = lax.psum_scatter(part, name, scatter_dimension=0, tiled=True)
    for name in gather:
        part = lax.all_gather(part, name, axis=0, tiled=True)
    return part


def body(
    node_feats,
    edge_feats,
    grad_nodes,
    grad_edges,
    sources,
    tile_blocks,
    offsets,
    edge_count,
    weights,
):
    extended = extended_2(node_feats, ((BULK, 0),), HALO)
    d_extended, edge_grads, grads = slab_backward(
        extended,
        edge_feats,
        grad_nodes,
        grad_edges,
        sources,
        tile_blocks,
        offsets,
        edge_count[0],
        weights,
    )
    own_rows = node_feats.shape[0]
    from_after = shifted(d_extended[:HALO].astype(jnp.bfloat16), BULK, -1).astype(jnp.float32)
    from_before = shifted(d_extended[HALO + own_rows :].astype(jnp.bfloat16), BULK, 1).astype(
        jnp.float32
    )
    own = d_extended[HALO : HALO + own_rows]
    own = own.at[:HALO].add(from_before)
    own = own.at[own_rows - HALO :].add(from_after)
    node_grads = own.astype(jnp.bfloat16)
    summed = reduce_grads(grads)
    factor = 1.0 / jnp.sqrt(jnp.float32(axis_count(DP + BULK) * edge_feats.shape[0]))
    return (node_grads, edge_grads, summed * factor)


def solution(mesh):
    devices = np.asarray(mesh.devices)
    shape = (2, devices.shape[0] // 4, 2, devices.shape[1] // 4, 4)
    fine = Mesh(devices.reshape(shape), DP + BULK)
    rows = P(DP + BULK, None)
    flat = P(DP + BULK)
    in_specs = (rows, rows, rows, rows, flat, flat, flat, flat, P())
    out_specs = (rows, rows, P(DP, None))
    return jax.shard_map(body, mesh=fine, in_specs=in_specs, out_specs=out_specs, check_vma=False)
```

```python
import jax
import jax.numpy as jnp
import numpy as np
from jax import lax
from jax.sharding import Mesh
from jax.sharding import PartitionSpec as P

HALO = 128


def extended_2(block, sides, width):
    for axis, dim in sides:
        count = axis_count(axis)
        forward = [(i, i + 1) for i in range(count - 1)]
        backward = [(target, source) for source, target in forward]
        low = lax.ppermute(
            lax.slice_in_dim(block, block.shape[dim] - width, None, axis=dim), axis, forward
        )
        high = lax.ppermute(lax.slice_in_dim(block, 0, width, axis=dim), axis, backward)
        block = jnp.concatenate([low, block, high], axis=dim)
    return block


def axis_count(axis):
    return int(np.prod([lax.axis_size(name) for name in axis]))


def shifted(value, axis, steps):
    count = axis_count(axis)
    initial, last = (max(0, -steps), min(count, count - steps))
    return lax.ppermute(value, axis, [(source, source + steps) for source in range(initial, last)])


def ln_core(values):
    middle = values - jnp.mean(values, -1, keepdims=True)
    spread = jnp.mean(middle * middle, -1, keepdims=True)
    return middle * lax.rsqrt(spread + 1e-05)


def ln_back(values, cotangent):
    unused, pull = jax.vjp(ln_core, values)
    return pull(cotangent)[0]


def silu_back(values, cotangent):
    sigma = jax.nn.sigmoid(values)
    return cotangent * sigma * (1.0 + values * (1.0 - sigma))


def left_dot(first, second):
    return lax.dot_general(
        first, second, (((0,), (0,)), ((), ())), preferred_element_type=jnp.float32
    )


def right_dot(first, second):
    return lax.dot_general(
        first, second, (((1,), (1,)), ((), ())), preferred_element_type=jnp.float32
    )


def slab_backward(
    extended, edge_feats, grad_nodes, grad_edges, sources, tile_blocks, offsets, count, weights
):
    width = weights.shape[1]
    own_rows = grad_nodes.shape[0]
    rim = (extended.shape[0] - own_rows) // 2
    ntiles = tile_blocks.shape[0]
    nedges = offsets.shape[0]
    tile = nedges // ntiles
    nblocks = own_rows // tile
    w_edge_one = weights[: 3 * width]
    w_edge_two = weights[3 * width : 4 * width]
    w_node_one = weights[4 * width : 6 * width]
    w_node_two = weights[6 * width :]
    dest = jnp.repeat(tile_blocks, tile) * tile + offsets
    live = (jnp.arange(nedges) < count).astype(jnp.float32)[:, None]
    joined = jnp.concatenate([extended[sources], extended[dest + rim], edge_feats], 1)
    act_one = jnp.dot(joined, w_edge_one, preferred_element_type=jnp.float32)
    hidden_one = jax.nn.silu(act_one).astype(jnp.bfloat16)
    act_two = jnp.dot(hidden_one, w_edge_two, preferred_element_type=jnp.float32)
    message = (ln_core(act_two) * live).astype(jnp.bfloat16)
    onehot = (offsets.reshape(ntiles, tile)[:, :, None] == jnp.arange(tile)[None, None, :]).astype(
        jnp.bfloat16
    )
    pertile = jnp.einsum(
        "tek,teh->tkh",
        onehot,
        message.reshape(ntiles, tile, width),
        preferred_element_type=jnp.float32,
    )
    gathered = jnp.zeros((nblocks, tile, width), jnp.float32).at[tile_blocks].add(pertile)
    aggregate = gathered.reshape(own_rows, width).astype(jnp.bfloat16)
    own_feats = extended[rim : rim + own_rows]
    joined_nodes = jnp.concatenate([own_feats, aggregate], 1)
    node_one = jnp.dot(joined_nodes, w_node_one, preferred_element_type=jnp.float32)
    node_hidden = jax.nn.silu(node_one).astype(jnp.bfloat16)
    node_two = jnp.dot(node_hidden, w_node_two, preferred_element_type=jnp.float32)
    d_node_two = ln_back(node_two, grad_nodes.astype(jnp.float32)).astype(jnp.bfloat16)
    g_node_two = left_dot(node_hidden, d_node_two)
    d_node_one = silu_back(node_one, right_dot(d_node_two, w_node_two)).astype(jnp.bfloat16)
    g_node_one = left_dot(joined_nodes, d_node_one)
    d_inputs = right_dot(d_node_one, w_node_one)
    d_aggregate = d_inputs[:, width:].astype(jnp.bfloat16)
    pulled = d_aggregate.reshape(nblocks, tile, width)[tile_blocks]
    d_message = jnp.einsum(
        "tek,tkh->teh", onehot, pulled, preferred_element_type=jnp.float32
    ).reshape(nedges, width)
    d_msg_total = live * (d_message + grad_edges.astype(jnp.float32))
    d_act_two = ln_back(act_two, d_msg_total).astype(jnp.bfloat16)
    g_edge_two = left_dot(hidden_one, d_act_two)
    d_act_one = silu_back(act_one, right_dot(d_act_two, w_edge_two)).astype(jnp.bfloat16)
    g_edge_one = left_dot(joined, d_act_one)
    d_joined = right_dot(d_act_one, w_edge_one)
    edge_grads = (grad_edges.astype(jnp.float32) + d_joined[:, 2 * width :]).astype(jnp.bfloat16)
    d_extended = jnp.zeros((extended.shape[0], width), jnp.float32)
    d_extended = d_extended.at[sources].add(d_joined[:, :width])
    d_extended = d_extended.at[dest + rim].add(d_joined[:, width : 2 * width])
    d_extended = d_extended.at[rim : rim + own_rows].add(
        grad_nodes.astype(jnp.float32) + d_inputs[:, :width]
    )
    grads = jnp.concatenate([g_edge_one, g_edge_two, g_node_one, g_node_two], 0)
    return (d_extended, edge_grads, grads)


DP = ("zh", "y", "c")
BULK = ("x", "zl")


def reduce_grads(grads):
    sizes = [lax.axis_size(name) for name in DP]
    rows = grads.shape[0] // int(np.prod(sizes))
    order = ("c", "y", "zh")
    blocks = grads.reshape(*sizes, rows, grads.shape[1])
    blocks = blocks.transpose([DP.index(name) for name in order] + [3, 4])
    part = blocks.reshape(grads.shape)
    part = lax.psum_scatter(part.astype(jnp.bfloat16), "c", scatter_dimension=0, tiled=True)
    part = part.astype(jnp.float32)
    for name in order[1:] + ("x", "zl"):
        part = lax.psum_scatter(part, name, scatter_dimension=0, tiled=True)
    for name in ("zl", "x"):
        part = lax.all_gather(part, name, axis=0, tiled=True)
    return part


def body(
    node_feats,
    edge_feats,
    grad_nodes,
    grad_edges,
    sources,
    tile_blocks,
    offsets,
    edge_count,
    weights,
):
    extended = extended_2(node_feats, ((BULK, 0),), HALO)
    d_extended, edge_grads, grads = slab_backward(
        extended,
        edge_feats,
        grad_nodes,
        grad_edges,
        sources,
        tile_blocks,
        offsets,
        edge_count[0],
        weights,
    )
    own_rows = node_feats.shape[0]
    from_after = shifted(d_extended[:HALO].astype(jnp.bfloat16), BULK, -1).astype(jnp.float32)
    from_before = shifted(d_extended[HALO + own_rows :].astype(jnp.bfloat16), BULK, 1).astype(
        jnp.float32
    )
    own = d_extended[HALO : HALO + own_rows]
    own = own.at[:HALO].add(from_before)
    own = own.at[own_rows - HALO :].add(from_after)
    node_grads = own.astype(jnp.bfloat16)
    summed = reduce_grads(grads)
    factor = 1.0 / jnp.sqrt(jnp.float32(axis_count(DP + BULK) * edge_feats.shape[0]))
    return (node_grads, edge_grads, summed * factor)


def solution(mesh):
    devices = np.asarray(mesh.devices)
    shape = (2, devices.shape[0] // 4, 2, devices.shape[1] // 4, 4)
    fine = Mesh(devices.reshape(shape), DP + BULK)
    rows = P(DP + BULK, None)
    flat = P(DP + BULK)
    in_specs = (rows, rows, rows, rows, flat, flat, flat, flat, P())
    out_specs = (rows, rows, P(DP, None))
    return jax.shard_map(body, mesh=fine, in_specs=in_specs, out_specs=out_specs, check_vma=False)
```

```python
import jax
import jax.numpy as jnp
import numpy as np
from jax import lax
from jax.sharding import Mesh
from jax.sharding import PartitionSpec as P

HALO = 128


def extended_2(block, sides, width):
    for axis, dim in sides:
        count = axis_count(axis)
        forward = [(i, i + 1) for i in range(count - 1)]
        backward = [(target, source) for source, target in forward]
        low = lax.ppermute(
            lax.slice_in_dim(block, block.shape[dim] - width, None, axis=dim), axis, forward
        )
        high = lax.ppermute(lax.slice_in_dim(block, 0, width, axis=dim), axis, backward)
        block = jnp.concatenate([low, block, high], axis=dim)
    return block


def axis_count(axis):
    return int(np.prod([lax.axis_size(name) for name in axis]))


def shifted(value, axis, steps):
    count = axis_count(axis)
    initial, last = (max(0, -steps), min(count, count - steps))
    return lax.ppermute(value, axis, [(source, source + steps) for source in range(initial, last)])


def ln_core(values):
    middle = values - jnp.mean(values, -1, keepdims=True)
    spread = jnp.mean(middle * middle, -1, keepdims=True)
    return middle * lax.rsqrt(spread + 1e-05)


def ln_back(values, cotangent):
    unused, pull = jax.vjp(ln_core, values)
    return pull(cotangent)[0]


def silu_back(values, cotangent):
    sigma = jax.nn.sigmoid(values)
    return cotangent * sigma * (1.0 + values * (1.0 - sigma))


def left_dot(first, second):
    return lax.dot_general(
        first, second, (((0,), (0,)), ((), ())), preferred_element_type=jnp.float32
    )


def right_dot(first, second):
    return lax.dot_general(
        first, second, (((1,), (1,)), ((), ())), preferred_element_type=jnp.float32
    )


def slab_backward(
    extended, edge_feats, grad_nodes, grad_edges, sources, tile_blocks, offsets, count, weights
):
    width = weights.shape[1]
    own_rows = grad_nodes.shape[0]
    rim = (extended.shape[0] - own_rows) // 2
    ntiles = tile_blocks.shape[0]
    nedges = offsets.shape[0]
    tile = nedges // ntiles
    nblocks = own_rows // tile
    w_edge_one = weights[: 3 * width]
    w_edge_two = weights[3 * width : 4 * width]
    w_node_one = weights[4 * width : 6 * width]
    w_node_two = weights[6 * width :]
    dest = jnp.repeat(tile_blocks, tile) * tile + offsets
    live = (jnp.arange(nedges) < count).astype(jnp.float32)[:, None]
    joined = jnp.concatenate([extended[sources], extended[dest + rim], edge_feats], 1)
    act_one = jnp.dot(joined, w_edge_one, preferred_element_type=jnp.float32)
    hidden_one = jax.nn.silu(act_one).astype(jnp.bfloat16)
    act_two = jnp.dot(hidden_one, w_edge_two, preferred_element_type=jnp.float32)
    message = (ln_core(act_two) * live).astype(jnp.bfloat16)
    onehot = (offsets.reshape(ntiles, tile)[:, :, None] == jnp.arange(tile)[None, None, :]).astype(
        jnp.bfloat16
    )
    pertile = jnp.einsum(
        "tek,teh->tkh",
        onehot,
        message.reshape(ntiles, tile, width),
        preferred_element_type=jnp.float32,
    )
    gathered = jnp.zeros((nblocks, tile, width), jnp.float32).at[tile_blocks].add(pertile)
    aggregate = gathered.reshape(own_rows, width).astype(jnp.bfloat16)
    own_feats = extended[rim : rim + own_rows]
    joined_nodes = jnp.concatenate([own_feats, aggregate], 1)
    node_one = jnp.dot(joined_nodes, w_node_one, preferred_element_type=jnp.float32)
    node_hidden = jax.nn.silu(node_one).astype(jnp.bfloat16)
    node_two = jnp.dot(node_hidden, w_node_two, preferred_element_type=jnp.float32)
    d_node_two = ln_back(node_two, grad_nodes.astype(jnp.float32)).astype(jnp.bfloat16)
    g_node_two = left_dot(node_hidden, d_node_two)
    d_node_one = silu_back(node_one, right_dot(d_node_two, w_node_two)).astype(jnp.bfloat16)
    g_node_one = left_dot(joined_nodes, d_node_one)
    d_inputs = right_dot(d_node_one, w_node_one)
    d_aggregate = d_inputs[:, width:].astype(jnp.bfloat16)
    pulled = d_aggregate.reshape(nblocks, tile, width)[tile_blocks]
    d_message = jnp.einsum(
        "tek,tkh->teh", onehot, pulled, preferred_element_type=jnp.float32
    ).reshape(nedges, width)
    d_msg_total = live * (d_message + grad_edges.astype(jnp.float32))
    d_act_two = ln_back(act_two, d_msg_total).astype(jnp.bfloat16)
    g_edge_two = left_dot(hidden_one, d_act_two)
    d_act_one = silu_back(act_one, right_dot(d_act_two, w_edge_two)).astype(jnp.bfloat16)
    g_edge_one = left_dot(joined, d_act_one)
    d_joined = right_dot(d_act_one, w_edge_one)
    edge_grads = (grad_edges.astype(jnp.float32) + d_joined[:, 2 * width :]).astype(jnp.bfloat16)
    d_extended = jnp.zeros((extended.shape[0], width), jnp.float32)
    d_extended = d_extended.at[sources].add(d_joined[:, :width])
    d_extended = d_extended.at[dest + rim].add(d_joined[:, width : 2 * width])
    d_extended = d_extended.at[rim : rim + own_rows].add(
        grad_nodes.astype(jnp.float32) + d_inputs[:, :width]
    )
    grads = jnp.concatenate([g_edge_one, g_edge_two, g_node_one, g_node_two], 0)
    return (d_extended, edge_grads, grads)


DP = ("zh", "y", "c")
BULK = ("x", "zl")


def reduce_grads(grads):
    sizes = [lax.axis_size(name) for name in DP]
    rows = grads.shape[0] // int(np.prod(sizes))
    order = ("c", "y", "zh")
    blocks = grads.reshape(*sizes, rows, grads.shape[1])
    blocks = blocks.transpose([DP.index(name) for name in order] + [3, 4])
    part = blocks.reshape(grads.shape)
    part = lax.psum_scatter(part.astype(jnp.bfloat16), "c", scatter_dimension=0, tiled=True)
    part = part.astype(jnp.float32)
    for name in order[1:] + ("x", "zl"):
        part = lax.psum_scatter(part, name, scatter_dimension=0, tiled=True)
    part = part.astype(jnp.bfloat16)
    for name in ("zl", "x"):
        part = lax.all_gather(part, name, axis=0, tiled=True)
    part = part.astype(jnp.float32)
    return part


def body(
    node_feats,
    edge_feats,
    grad_nodes,
    grad_edges,
    sources,
    tile_blocks,
    offsets,
    edge_count,
    weights,
):
    extended = extended_2(node_feats, ((BULK, 0),), HALO)
    d_extended, edge_grads, grads = slab_backward(
        extended,
        edge_feats,
        grad_nodes,
        grad_edges,
        sources,
        tile_blocks,
        offsets,
        edge_count[0],
        weights,
    )
    own_rows = node_feats.shape[0]
    from_after = shifted(d_extended[:HALO].astype(jnp.bfloat16), BULK, -1).astype(jnp.float32)
    from_before = shifted(d_extended[HALO + own_rows :].astype(jnp.bfloat16), BULK, 1).astype(
        jnp.float32
    )
    own = d_extended[HALO : HALO + own_rows]
    own = own.at[:HALO].add(from_before)
    own = own.at[own_rows - HALO :].add(from_after)
    node_grads = own.astype(jnp.bfloat16)
    summed = reduce_grads(grads)
    factor = 1.0 / jnp.sqrt(jnp.float32(axis_count(DP + BULK) * edge_feats.shape[0]))
    return (node_grads, edge_grads, summed * factor)


def solution(mesh):
    devices = np.asarray(mesh.devices)
    shape = (2, devices.shape[0] // 4, 2, devices.shape[1] // 4, 4)
    fine = Mesh(devices.reshape(shape), DP + BULK)
    rows = P(DP + BULK, None)
    flat = P(DP + BULK)
    in_specs = (rows, rows, rows, rows, flat, flat, flat, flat, P())
    out_specs = (rows, rows, P(DP, None))
    return jax.shard_map(body, mesh=fine, in_specs=in_specs, out_specs=out_specs, check_vma=False)
```
